32 devices in a mesh: gx: 4 (over x, core), gy: 8 (over z, y).
Axes of the slice: x: 2, y: 2, z: 4, core: 2. Of those that a mesh axis runs over, the one named last changes fastest.
Arguments:
- features: bfloat16 [4, 128, 128, 128, 64], P(None, 'gx', 'gy'), may hold values from -6 to 6
- spectral_weight: bfloat16 [2, 32, 32, 32, 64, 64], P(None, None, 'gx', 'gy'), may hold values from -3 to 3
- skip_weight: bfloat16 [64, 64], replicated, may hold values from -0.75 to 0.75
- skip_bias: float32 [64], replicated, may hold values from -3 to 3
- mlp_in: bfloat16 [64, 256], replicated, may hold values from -0.75 to 0.75
- mlp_in_bias: float32 [256], replicated, may hold values from -3 to 3
- mlp_out: bfloat16 [256, 64], replicated, may hold values from -0.375 to 0.375
Outputs:
- layer_out: bfloat16 [4, 128, 128, 128, 64], P(None, 'gx', 'gy')
The draws below stay inside these ranges and needn't reach their ends.
All inputs are finite; a program needn't handle non-finite values.
Results may differ from the reference program's by a relative error of at most 0.015.
Values may be sent and summed in bfloat16 or wider, within the bound.
A program may use at most 384 MiB of HBM per device.

```python
import math
import jax
import jax.numpy as jnp
from jax import lax

GRID = 128
MODES = 32
CH = 64
MLP_WIDTH = 256
BATCH = 4


def block_scale(stream_key, dims, split, least, high):
    factor_of, own = 1.0, jax.random.fold_in(stream_key, 6)
    for dim, blocks in split:
        draws = jnp.exp(jax.random.uniform(jax.random.fold_in(own, dim), (blocks,), jnp.float32, least / len(split), high / len(split)))
        factor_of = factor_of * jnp.repeat(draws, dims[dim] // blocks).reshape([-1 if axis == dim else 1 for axis in range(len(dims))])
    return factor_of


def noise(own_key, extent, width, most, cuts=(), kind=jnp.bfloat16):
    values = width * jax.random.normal(own_key, extent, jnp.float32)
    if cuts:
        values = values * block_scale(own_key, extent, cuts, -0.22, 0.18)
    return jnp.clip(values, -most, most).astype(kind)


def setup_inputs(seed: int = 0) -> dict:
    arg_keys = jax.random.split(jax.random.key(seed), 8)
    features = noise(arg_keys[0], (BATCH, GRID, GRID, GRID, CH), 1.0, 6.0, ((1, 4), (2, 8)))
    spectral_weight = noise(arg_keys[1], (2, MODES, MODES, MODES, CH, CH), (CH // 16) ** -0.5, 3.0, ((2, 4), (3, 8)))
    skip_weight = noise(arg_keys[2], (CH, CH), CH ** -0.5, 0.75)
    skip_bias = noise(arg_keys[3], (CH,), 0.5, 3.0, (), jnp.float32)
    mlp_in = noise(arg_keys[4], (CH, MLP_WIDTH), CH ** -0.5, 0.75)
    mlp_in_bias = noise(arg_keys[5], (MLP_WIDTH,), 0.5, 3.0, (), jnp.float32)
    mlp_out = noise(arg_keys[6], (MLP_WIDTH, CH), MLP_WIDTH ** -0.5, 0.375)
    return {"features": features, "spectral_weight": spectral_weight, "skip_weight": skip_weight, "skip_bias": skip_bias, "mlp_in": mlp_in, "mlp_in_bias": mlp_in_bias, "mlp_out": mlp_out}


def wave_tables(length, retained, wrapped):
    position = jnp.arange(length, dtype=jnp.int32)
    ordinal = jnp.arange(retained, dtype=jnp.int32)
    if wrapped:
        ordinal = jnp.where(ordinal < retained // 2, ordinal, ordinal + (length - retained))
    phases = position[:, None] * ordinal[None, :] % length
    angles = phases.astype(jnp.float32) * (2.0 * math.pi / length)
    scaling = 1.0 / math.sqrt(length)
    return ((jnp.cos(angles) * scaling).astype(jnp.bfloat16), (jnp.sin(angles) * scaling).astype(jnp.bfloat16))

def forward_spin(cosine, sine_table):
    upper_half = jnp.stack([cosine, -sine_table], axis=1)
    lower_half = jnp.stack([sine_table, cosine], axis=1)
    return jnp.stack([upper_half, lower_half], axis=0)

def inverse_spin(cosine, sine_table):
    cos_t = cosine.T
    sin_t = sine_table.T
    upper_half = jnp.stack([cos_t, sin_t], axis=1)
    lower_half = jnp.stack([-sin_t, cos_t], axis=1)
    return jnp.stack([upper_half, lower_half], axis=0)

def z_inverse(cosine, sine_table):
    retained = cosine.shape[1]
    ordinal = jnp.arange(retained, dtype=jnp.int32)
    factor = jnp.where(ordinal == 0, 1.0, 2.0).astype(jnp.bfloat16)[:, None]
    return jnp.stack([cosine.T * factor, -(sine_table.T * factor)], axis=0)

def pointwise(values, spectral, skip_weight, skip_bias, mlp_in, mlp_in_bias, mlp_out):
    shape_kept = values.shape
    flat = values.reshape(-1, shape_kept[-1])
    pre = spectral.reshape(flat.shape) + jnp.dot(flat, skip_weight, preferred_element_type=jnp.float32) + skip_bias
    hidden = jax.nn.gelu(pre).astype(jnp.bfloat16)
    expanded = jax.nn.gelu(jnp.dot(hidden, mlp_in, preferred_element_type=jnp.float32) + mlp_in_bias).astype(jnp.bfloat16)
    result = hidden.astype(jnp.float32) + jnp.dot(expanded, mlp_out, preferred_element_type=jnp.float32)
    return result.astype(jnp.bfloat16).reshape(shape_kept)

def reference(features, spectral_weight, skip_weight, skip_bias, mlp_in, mlp_in_bias, mlp_out):
    cos_z, sin_z = wave_tables(GRID, MODES, False)
    cos_y, sin_y = wave_tables(GRID, MODES, True)
    z_table = jnp.stack([cos_z, -sin_z], axis=1).astype(jnp.float32)
    forward_table = forward_spin(cos_y, sin_y).astype(jnp.float32)
    backward_table = inverse_spin(cos_y, sin_y).astype(jnp.float32)
    z_back = z_inverse(cos_z, sin_z).astype(jnp.float32)
    weights = spectral_weight.astype(jnp.float32)

    def tail_plane(planes):
        return pointwise(planes[0], planes[1], skip_weight, skip_bias, mlp_in, mlp_in_bias, mlp_out)

    def one_sample(sample):
        z_spec = jnp.einsum('xyzc,zpk->pxykc', sample.astype(jnp.float32), z_table).astype(jnp.bfloat16)
        y_spec = jnp.einsum('pxyzc,pyqk->qxkzc', z_spec.astype(jnp.float32), forward_table).astype(jnp.bfloat16)
        x_spec = jnp.einsum('pxyzc,pxqk->qkyzc', y_spec.astype(jnp.float32), forward_table).astype(jnp.bfloat16)
        products = jnp.einsum('pxyzi,wxyzio->pwxyzo', x_spec.astype(jnp.float32), weights)
        mixed_modes = jnp.stack([products[0, 0] - products[1, 1], products[0, 1] + products[1, 0]]).astype(jnp.bfloat16)
        x_back = jnp.einsum('pkyzc,pkqx->qxyzc', mixed_modes.astype(jnp.float32), backward_table).astype(jnp.bfloat16)
        y_back = jnp.einsum('pxkzc,pkqy->qxyzc', x_back.astype(jnp.float32), backward_table).astype(jnp.bfloat16)
        spectral = jnp.einsum('pxykc,pkz->xyzc', y_back.astype(jnp.float32), z_back)
        return lax.map(tail_plane, (sample, spectral))
    return lax.map(one_sample, features)
```

```python
import functools
import math

import jax
import jax.numpy as jnp
from jax import lax
from jax.experimental import pallas as pl
from jax.experimental.pallas import tpu as pltpu
from jax.sharding import PartitionSpec as P

MODES = 32
GROUPS = 2
BF = jnp.bfloat16
F32 = jnp.float32


def wave_tables(length, retained, wrapped):
    position = jnp.arange(length, dtype=jnp.int32)
    ordinal = jnp.arange(retained, dtype=jnp.int32)
    if wrapped:
        ordinal = jnp.where(ordinal < retained // 2, ordinal, ordinal + (length - retained))
    phases = position[:, None] * ordinal[None, :] % length
    angles = phases.astype(jnp.float32) * (2.0 * math.pi / length)
    scaling = 1.0 / math.sqrt(length)
    return (
        (jnp.cos(angles) * scaling).astype(jnp.bfloat16),
        (jnp.sin(angles) * scaling).astype(jnp.bfloat16),
    )


def forward_spin(cosine, sine_table):
    upper_half = jnp.stack([cosine, -sine_table], axis=1)
    lower_half = jnp.stack([sine_table, cosine], axis=1)
    return jnp.stack([upper_half, lower_half], axis=0)


def inverse_spin(cosine, sine_table):
    cos_t = cosine.T
    sin_t = sine_table.T
    upper_half = jnp.stack([cos_t, sin_t], axis=1)
    lower_half = jnp.stack([-sin_t, cos_t], axis=1)
    return jnp.stack([upper_half, lower_half], axis=0)


def gelu(v):
    half = 0.5 * v
    k0 = math.sqrt(2.0 / math.pi)
    t = jnp.tanh(v * (k0 + (k0 * 0.044715) * (v * v)))
    return half + half * t


def z_kernel(n, f_ref, t_ref, *outs):
    rows_y = f_ref.shape[2]
    ch, length = f_ref.shape[3], f_ref.shape[4]
    table = t_ref[...]
    r = table.shape[0] // n
    res = []
    for y in range(rows_y):
        block = f_ref[0, :, y].reshape(2 * ch, length)
        res.append(
            lax.dot_general(table, block, (((1,), (1,)), ((), ())), preferred_element_type=F32)
        )
    for i in range(n):
        rows = jnp.concatenate([v[i * r : (i + 1) * r] for v in res], axis=0)
        outs[i][0, 0] = rows.astype(BF)


def z_forward(feats, table, first, count, n):
    _, rows_x, rows_y, ch, length = feats.shape
    pairs = rows_x // 2
    rows = rows_y * table.shape[0] // n
    out = jax.ShapeDtypeStruct((count, pairs, rows, 2 * ch), BF)
    spec = pl.BlockSpec((1, 1, rows, 2 * ch), lambda b, a: (b, a, 0, 0))
    return pl.pallas_call(
        functools.partial(z_kernel, n),
        grid=(count, pairs),
        in_specs=[
            pl.BlockSpec((1, 2, rows_y, ch, length), lambda b, a: (b + first, a, 0, 0, 0)),
            pl.BlockSpec(table.shape, lambda b, a: (0, 0)),
        ],
        out_specs=[spec] * n,
        out_shape=[out] * n,
        cost_estimate=pl.CostEstimate(
            flops=2 * count * rows_x * rows_y * ch * length * 64,
            bytes_accessed=3 * count * rows_x * rows_y * ch * length,
            transcendentals=0,
        ),
        name="z_forward",
    )(feats, table)


def y_kernel(n, m_ref, *refs):
    ins, out = refs[:n], refs[n]
    total = None
    for i in range(n):
        part = jnp.dot(m_ref[i], ins[i][0, 0], preferred_element_type=F32)
        total = part if total is None else total + part
    g, rows = out.shape[1], out.shape[3]
    for j in range(g):
        out[0, j, 0] = total[j * rows : (j + 1) * rows].astype(BF)


def y_forward(parts, mats, g):
    n = len(parts)
    count, pairs, rows, lanes = parts[0].shape
    outs = mats.shape[1]
    return pl.pallas_call(
        functools.partial(y_kernel, n),
        grid=(count, pairs),
        in_specs=[pl.BlockSpec(mats.shape, lambda b, a: (0, 0, 0))]
        + [pl.BlockSpec((1, 1, rows, lanes), lambda b, a: (b, a, 0, 0))] * n,
        out_specs=pl.BlockSpec((1, g, 1, outs // g, lanes), lambda b, a: (b, 0, a, 0, 0)),
        out_shape=jax.ShapeDtypeStruct((count, g, pairs, outs // g, lanes), BF),
        cost_estimate=pl.CostEstimate(
            flops=2 * count * pairs * rows * n * lanes * outs,
            bytes_accessed=4 * count * pairs * lanes * (rows * n),
            transcendentals=0,
        ),
        name="y_forward",
    )(mats, *parts)


def yb_kernel(n, m_ref, x_ref, *outs):
    g = x_ref.shape[1]
    block = jnp.concatenate([x_ref[0, j, 0] for j in range(g)], axis=0)
    for i in range(n):
        outs[i][0, 0] = jnp.dot(m_ref[i], block, preferred_element_type=F32).astype(BF)


def y_backward(lines, mats):
    n, rows, _ = mats.shape
    count, g, pairs, each, lanes = lines.shape
    return pl.pallas_call(
        functools.partial(yb_kernel, n),
        grid=(count, pairs),
        in_specs=[
            pl.BlockSpec(mats.shape, lambda b, a: (0, 0, 0)),
            pl.BlockSpec((1, g, 1, each, lanes), lambda b, a: (b, 0, a, 0, 0)),
        ],
        out_specs=[pl.BlockSpec((1, 1, rows, lanes), lambda b, a: (b, a, 0, 0))] * n,
        out_shape=[jax.ShapeDtypeStruct((count, pairs, rows, lanes), BF)] * n,
        cost_estimate=pl.CostEstimate(
            flops=2 * count * pairs * rows * n * lanes * g * each,
            bytes_accessed=4 * count * pairs * lanes * (rows * n),
            transcendentals=0,
        ),
        name="y_backward",
    )(mats, lines)


def tail_kernel(n, r, step, f_ref, zb_ref, ws_ref, bs_ref, wi_ref, bi_ref, wo_ref, *refs):
    ins, out = refs[:n], refs[-1]
    ch, length = f_ref.shape[3], f_ref.shape[4]
    rows_y = f_ref.shape[2]

    def body(s, carry):
        chunk = [
            ins[i][0, 0, pl.ds(pl.multiple_of(s * (step * r), step * r), step * r), :].astype(F32)
            for i in range(n)
        ]
        spec, feat = [], []
        for k in range(step):
            modes = jnp.concatenate([v[k * r : (k + 1) * r] for v in chunk], axis=0).astype(BF)
            sp = lax.dot_general(
                modes, zb_ref[...], (((0,), (0,)), ((), ())), preferred_element_type=F32
            )
            for h in range(2):
                spec.append(sp[h * ch : (h + 1) * ch])
                feat.append(f_ref[0, h, s * step + k])
        pre = (
            jnp.concatenate(spec, axis=1)
            + jnp.dot(ws_ref[...], jnp.concatenate(feat, axis=1), preferred_element_type=F32)
            + bs_ref[...]
        )
        hidden32 = gelu(pre)
        hidden = hidden32.astype(BF)
        wide = jnp.dot(wi_ref[...], hidden, preferred_element_type=F32) + bi_ref[...]
        expanded = gelu(wide).astype(BF)
        res = hidden.astype(F32) + jnp.dot(wo_ref[...], expanded, preferred_element_type=F32)
        res = res.astype(BF)
        for k in range(step):
            for h in range(2):
                at = (k * 2 + h) * length
                out[0, h, s * step + k] = res[:, at : at + length]
        return carry

    lax.fori_loop(0, rows_y // step, body, 0)


def tail(feats, parts, table, ws, bs, wi, bi, wo, first, previous):
    n = len(parts)
    _, rows_x, rows_y, ch, length = feats.shape
    count, pairs, rows, lanes = parts[0].shape
    r = rows // rows_y
    step = max(1, 16 // r)
    fspec = pl.BlockSpec((1, 2, rows_y, ch, length), lambda b, a: (b + first, a, 0, 0, 0))
    small = [table, ws, bs, wi, bi, wo]
    args = [feats, *small, *parts]
    in_specs = (
        [fspec]
        + [pl.BlockSpec(v.shape, lambda b, a: (0, 0)) for v in small]
        + [pl.BlockSpec((1, 1, rows, lanes), lambda b, a: (b, a, 0, 0))] * n
    )
    aliases = {}
    if previous is not None:
        aliases = {len(args): 0}
        args.append(previous)
        in_specs.append(pl.BlockSpec(memory_space=pl.ANY))
    cells = count * rows_x * rows_y * length
    return pl.pallas_call(
        functools.partial(tail_kernel, n, r, step),
        grid=(count, pairs),
        in_specs=in_specs,
        out_specs=fspec,
        out_shape=jax.ShapeDtypeStruct(feats.shape, BF),
        input_output_aliases=aliases,
        cost_estimate=pl.CostEstimate(
            flops=2 * cells * ch * 640, bytes_accessed=5 * cells * ch, transcendentals=cells * 320
        ),
        name="tail",
    )(*args)


def exchange(parts, n):
    return [parts[0]] + [
        lax.ppermute(parts[i], "gy", [(d, (d + i) % n) for d in range(n)]) for i in range(1, n)
    ]


def shards(g, n, features, spectral_weight, skip_weight, skip_bias, mlp_in, mlp_in_bias, mlp_out):
    samples, rows_x, rows_y, length, ch = features.shape
    pairs = rows_x // 2
    kb, yb = MODES // n, MODES // g
    me = lax.axis_index("gy")
    order = jnp.arange(n, dtype=jnp.int32)
    to = (me + order) % n
    source = (me - order + n) % n
    feats = jnp.swapaxes(features, 3, 4)

    cos_z, sin_z = wave_tables(length, MODES, False)
    cos_y, sin_y = wave_tables(length, MODES, True)
    forward_table = forward_spin(cos_y, sin_y)
    backward_table = inverse_spin(cos_y, sin_y)

    z_rows = jnp.stack([cos_z, -sin_z], axis=0).transpose(0, 2, 1)
    z_rows = z_rows.reshape(2, n, kb, length).transpose(1, 0, 2, 3)
    z_table = z_rows[to].reshape(2 * MODES, length)
    factor = jnp.where(jnp.arange(MODES) == 0, 1.0, 2.0).astype(BF)[:, None]
    zi = jnp.stack([cos_z.T * factor, -(sin_z.T * factor)], axis=0)
    zi = zi.reshape(2, n, kb, length).transpose(1, 0, 2, 3)
    zi_table = zi[source].reshape(2 * MODES, length)

    eye = jnp.eye(kb, dtype=BF)
    ft = forward_table.reshape(2, n, rows_y, 2, g, yb)
    fm = jnp.einsum("psyqgk,zw->sgqkzypw", ft, eye)
    fm = fm.reshape(n, 2 * MODES * kb, rows_y * 2 * kb)[source]
    bt = backward_table.reshape(2, g, yb, 2, n, rows_y)
    bm = jnp.einsum("pgkqsy,zw->syqzgpkw", bt, eye)
    bm = bm.reshape(n, rows_y * 2 * kb, 2 * MODES * kb)[to]
    fm, bm = lax.optimization_barrier((fm, bm))

    xf = forward_table.reshape(2, g, pairs, 2, 2, MODES)
    xb = backward_table.reshape(2, MODES, 2, g, pairs, 2)

    ws, wi, wo = skip_weight.T, mlp_in.T, mlp_out.T
    bs, bi = skip_bias[:, None], mlp_in_bias[:, None]

    groups = GROUPS if samples % GROUPS == 0 else 1
    count = samples // groups
    result = None
    landed = []
    for j in range(groups):
        landed.append(exchange(z_forward(feats, z_table, j * count, count, n), n))
    back = []
    for j in range(groups):
        y_spec = y_forward(landed[j], fm, g)
        lines = lax.all_to_all(y_spec, "gx", split_axis=1, concat_axis=1, tiled=True)
        lines = lines.reshape(count, g, pairs, 2, yb, kb, 2, ch)
        x_spec = jnp.einsum(
            "bsapyzvc,psavqk->qbkyzc", lines, xf, preferred_element_type=F32
        ).astype(BF)
        products = jnp.einsum(
            "pbxyzi,wxyzio->pwbxyzo", x_spec, spectral_weight, preferred_element_type=F32
        )
        mixed = jnp.stack(
            [products[0, 0] - products[1, 1], products[0, 1] + products[1, 0]]
        ).astype(BF)
        x_back = jnp.einsum(
            "pbkyzc,pkqsav->bsaqyzvc", mixed, xb, preferred_element_type=F32
        ).astype(BF)
        x_back = x_back.reshape(count, g, pairs, 2 * yb * kb, 2 * ch)
        x_back = lax.all_to_all(x_back, "gx", split_axis=1, concat_axis=1, tiled=True)
        back.append(exchange(y_backward(x_back, bm), n))
    for j in range(groups):
        result = tail(feats, back[j], zi_table, ws, bs, wi, bi, wo, j * count, result)
    return jnp.swapaxes(result, 3, 4)


def solution(mesh):
    return jax.shard_map(
        functools.partial(shards, mesh.shape["gx"], mesh.shape["gy"]),
        mesh=mesh,
        in_specs=(
            P(None, "gx", "gy", None, None),
            P(None, None, "gx", "gy", None, None),
            P(),
            P(),
            P(),
            P(),
            P(),
        ),
        out_specs=P(None, "gx", "gy", None, None),
        check_vma=False,
    )
```
